32 devices in a mesh: grp: 2 (over x), row: 8 (over z, y), col: 2 (over core).
Axes of the slice: x: 2, y: 2, z: 4, core: 2. Of those that a mesh axis runs over, the one named last changes fastest.
Arguments:
- query_window: bfloat16 [16, 8, 128, 1280], P(('grp', 'row'), 'col'), parts along dimension 0, may hold values from -80 to 80
- key_window: bfloat16 [16, 8, 128, 1280], P(('grp', 'row'), 'col'), parts along dimension 0, may hold values from -9 to 9
- value_window: bfloat16 [16, 8, 128, 1280], P(('grp', 'row'), 'col'), parts along dimension 0, may hold values from -6 to 6
- query_index: bfloat16 [16, 8, 128, 1280], P(('grp', 'row'), 'col'), parts along dimension 0, may hold values from -80 to 80
- key_index: bfloat16 [16, 8, 128, 1280], P(('grp', 'row'), 'col'), parts along dimension 0, may hold values from -9 to 9
- proj_weight: bfloat16 [1280, 1024], replicated, may hold values from -0.5 to 0.5
- proj_bias: float32 [1024], replicated, may hold values from -3 to 3
- first_kernel: bfloat16 [3, 3, 256, 256], replicated, may hold values from -0.125 to 0.125
- first_bias: float32 [256], replicated, may hold values from -3 to 3
- second_kernel: bfloat16 [3, 3, 256, 256], replicated, may hold values from -0.125 to 0.125
- second_bias: float32 [256], replicated, may hold values from -3 to 3
Outputs:
- fine_field: bfloat16 [256, 256, 256], P(('grp', 'row'), 'col'), parts along dimension 0
The draws below stay inside these ranges and needn't reach their ends.
There are 2 independent parts, one for each index of `grp`. The reference program is written for one: setup_inputs(seed, part) draws one part's arguments, and reference() takes and returns one part's arrays. A program takes and returns all parts, laid end to end along the dimension named above; an argument that names none is the same for every part. Nothing has to cross between parts.
All inputs are finite; a program needn't handle non-finite values.
Results may differ from the reference program's by a relative error of at most 0.0048.
Values may be sent and summed in bfloat16 or wider, within the bound.
A program may use at most 64 MiB of HBM per device.

```python
import math
import jax
import jax.numpy as jnp
from jax import lax

HEADS = 8
HEAD_DIM = 160
CHANNELS = 256
TILE_ROWS = 8
TILE_COLS = 16
INNER = 1280
WIN_TOKENS = 128
WIN_ROWS = 8
WIN_COLS = 8


def paired_draw(key):
    layout = (WIN_ROWS * WIN_COLS, WIN_TOKENS, HEADS, HEAD_DIM)
    key_draw = 1.41 * jax.random.truncated_normal(jax.random.fold_in(key, 11), -6.0, 6.0, layout, jnp.float32)
    query_draw = 1.41 * jax.random.truncated_normal(jax.random.fold_in(key, 12), -6.0, 6.0, layout, jnp.float32)
    final = (WIN_ROWS, WIN_COLS, WIN_TOKENS, HEADS * HEAD_DIM)
    return (query_draw.reshape(final).astype(jnp.bfloat16), key_draw.reshape(final).astype(jnp.bfloat16))


def draw_query_window(key, part):
    return paired_draw(jax.random.fold_in(key, 101))[0]


def draw_key_window(key, part):
    return paired_draw(jax.random.fold_in(key, 101))[1]


def draw_query_index(key, part):
    return paired_draw(jax.random.fold_in(key, 202))[0]


def draw_key_index(key, part):
    return paired_draw(jax.random.fold_in(key, 202))[1]


def steps_of(stream_key, dims, pieces, low, top_value):
    loudness = 1.0
    for position, parts in pieces:
        heights = jax.random.uniform(jax.random.fold_in(jax.random.fold_in(stream_key, 6), position), (parts,), jnp.float32, low / len(pieces), top_value / len(pieces))
        loudness = loudness * jnp.repeat(jnp.exp(heights), dims[position] // parts).reshape((-1,) + (1,) * (len(dims) - 1 - position))
    return loudness


def scatter_about(stream_key, extent, spread, reach, cuts=(), held_as=jnp.bfloat16):
    drawn = spread * jax.random.normal(stream_key, extent, jnp.float32)
    if cuts:
        drawn = drawn * steps_of(stream_key, extent, cuts, -0.22, 0.18)
    return jnp.clip(drawn, -reach, reach).astype(held_as)


def setup_inputs(seed: int = 0, part: int = 0) -> dict:
    keys = jax.random.split(jax.random.key(seed), 12)
    part_keys = jax.random.split(jax.random.fold_in(keys[11], part), 12)
    return {
        "query_window": draw_query_window(jax.random.fold_in(jax.random.fold_in(keys[11], part), 71), part),
        "key_window": draw_key_window(jax.random.fold_in(jax.random.fold_in(keys[11], part), 71), part),
        "value_window": scatter_about(part_keys[2], (WIN_ROWS, WIN_COLS, WIN_TOKENS, INNER), 1.0, 6.0, ((0, 8), (1, 2))),
        "query_index": draw_query_index(jax.random.fold_in(jax.random.fold_in(keys[11], part), 71), part),
        "key_index": draw_key_index(jax.random.fold_in(jax.random.fold_in(keys[11], part), 71), part),
        "proj_weight": scatter_about(keys[5], (INNER, 4 * CHANNELS), (INNER // 8) ** -0.5, 0.5),
        "proj_bias": scatter_about(keys[6], (4 * CHANNELS,), 0.5, 3.0, (), jnp.float32),
        "first_kernel": scatter_about(keys[7], (3, 3, CHANNELS, CHANNELS), (9 * CHANNELS) ** -0.5, 0.125),
        "first_bias": scatter_about(keys[8], (CHANNELS,), 0.5, 3.0, (), jnp.float32),
        "second_kernel": scatter_about(keys[9], (3, 3, CHANNELS, CHANNELS), (9 * CHANNELS) ** -0.5, 0.125),
        "second_bias": scatter_about(keys[10], (CHANNELS,), 0.5, 3.0, (), jnp.float32),
    }


def attend(queries, key_rows, values):
    scores = jnp.einsum('blhd,bmhd->bhlm', queries.astype(jnp.float32), key_rows.astype(jnp.float32)) / math.sqrt(HEAD_DIM)
    highest = lax.optimization_barrier(jnp.max(scores, axis=-1, keepdims=True))
    raised = jnp.exp(scores - highest)
    weights = (raised / lax.optimization_barrier(jnp.sum(raised, axis=-1, keepdims=True))).astype(jnp.bfloat16)
    mixed = jnp.einsum('bhlm,bmhd->blhd', weights.astype(jnp.float32), values.astype(jnp.float32))
    return mixed.astype(jnp.bfloat16)

def convolve(image, kernel, bias):
    height, breadth, depth = image.shape
    padded = jnp.pad(image, ((1, 1), (1, 1), (0, 0)))
    total = jnp.zeros((height * breadth, kernel.shape[-1]), jnp.float32)
    for row_shift in range(3):
        for col_shift in range(3):
            cells = padded[row_shift:row_shift + height, col_shift:col_shift + breadth].reshape(-1, depth)
            total = total + jnp.dot(cells, kernel[row_shift, col_shift], preferred_element_type=jnp.float32)
    return (total + bias).reshape(height, breadth, -1)

def reference(query_window, key_window, value_window, query_index, key_index, proj_weight, proj_bias, first_kernel, first_bias, second_kernel, second_bias):
    layout = (WIN_ROWS * WIN_COLS, WIN_TOKENS, HEADS, HEAD_DIM)
    window_out = attend(query_window.reshape(layout), key_window.reshape(layout), value_window.reshape(layout))
    index_out = attend(jnp.swapaxes(query_index.reshape(layout), 0, 1), jnp.swapaxes(key_index.reshape(layout), 0, 1), jnp.swapaxes(window_out, 0, 1))
    index_rows = jnp.swapaxes(index_out, 0, 1).reshape(-1, HEADS * HEAD_DIM)
    projected = (jnp.dot(index_rows, proj_weight, preferred_element_type=jnp.float32) + proj_bias).astype(jnp.bfloat16)
    grouped = projected.reshape(WIN_ROWS, WIN_COLS, TILE_ROWS, TILE_COLS, 2, 2, CHANNELS)
    shuffled = jnp.transpose(grouped, (0, 2, 4, 1, 3, 5, 6)).reshape(WIN_ROWS * TILE_ROWS * 2, WIN_COLS * TILE_COLS * 2, CHANNELS)
    activated = jax.nn.gelu(convolve(shuffled, first_kernel, first_bias)).astype(jnp.bfloat16)
    return convolve(activated, second_kernel, second_bias).astype(jnp.bfloat16)
```

```python
import functools
import math

import jax
import jax.numpy as jnp
from jax import lax
from jax.experimental import pallas as pl
from jax.experimental.pallas import tpu as pltpu
from jax.sharding import PartitionSpec as P

HEADS = 8
HEAD_DIM = 160
CHANNELS = 256
TILE_ROWS = 8
TILE_COLS = 16
LANES = 128


def extended(value, sides, width):
    for axis, dim in sides:
        size, length = (lax.axis_size(axis), value.shape[dim])
        up = [(i, (i + 1) % size) for i in range(size - 1)]
        down = [(j, i) for i, j in up]
        last = lax.slice_in_dim(value, length - width, length, axis=dim)
        first = lax.slice_in_dim(value, 0, width, axis=dim)
        before = lax.ppermute(last, axis, up)
        after = lax.ppermute(first, axis, down)
        value = jnp.concatenate([before, value, after], axis=dim)
    return value


def softmax_rows(scores):
    highest = jnp.max(scores, axis=-1, keepdims=True)
    raised = jnp.exp(scores - highest)
    return (raised / jnp.sum(raised, axis=-1, keepdims=True)).astype(jnp.bfloat16)


def window_attend(queries, key_rows, values):
    scores = jnp.einsum(
        "blhd,bmhd->bhlm", queries, key_rows, preferred_element_type=jnp.float32
    ) / math.sqrt(HEAD_DIM)
    weights = softmax_rows(scores)
    return jnp.einsum(
        "bhlm,bmhd->blhd", weights, values, preferred_element_type=jnp.float32
    ).astype(jnp.bfloat16)


def index_attend(queries, key_rows, values):
    scores = jnp.einsum(
        "lbhd,mbhd->bhlm", queries, key_rows, preferred_element_type=jnp.float32
    ) / math.sqrt(HEAD_DIM)
    weights = softmax_rows(scores)
    return jnp.einsum(
        "bhlm,mbhd->lbhd", weights, values, preferred_element_type=jnp.float32
    ).astype(jnp.bfloat16)


def convolve(image, kernel, bias):
    height, breadth, depth = image.shape
    padded = extended(image, (("row", 0), ("col", 1)), 1)
    total = jnp.zeros((height * breadth, kernel.shape[-1]), jnp.float32)
    for row_shift in range(3):
        for col_shift in range(3):
            cells = padded[row_shift : row_shift + height, col_shift : col_shift + breadth].reshape(
                -1, depth
            )
            total = total + jnp.dot(
                cells, kernel[row_shift, col_shift], preferred_element_type=jnp.float32
            )
    return (total + bias).reshape(height, breadth, -1)


def attend_heads(queries, key_part, value_part, same):
    rows, features = queries.shape
    head_dim = features // HEADS
    factor = math.log2(math.e) / math.sqrt(head_dim)
    blocks = [None] * (features // LANES)
    for head in range(HEADS):
        low, high = (head * head_dim, (head + 1) * head_dim)
        start, stop = (low // LANES * LANES, -(-high // LANES) * LANES)
        lane = lax.broadcasted_iota(jnp.int32, (rows, stop - start), 1) + start
        inside = (lane >= low) & (lane < high)
        part = queries[:, start:stop]
        part = jnp.where(inside, part, jnp.zeros_like(part))
        scores = lax.dot_general(
            part,
            key_part(start, stop),
            (((1,), (1,)), ((), ())),
            preferred_element_type=jnp.float32,
        )
        if same is not None:
            scores = jnp.where(same, scores, -1e30)
        highest = jnp.max(scores, axis=-1, keepdims=True)
        raised = jnp.exp2((scores - highest) * factor)
        weights = (raised * (1.0 / jnp.sum(raised, axis=-1, keepdims=True))).astype(jnp.bfloat16)
        mixed = jnp.dot(weights, value_part(start, stop), preferred_element_type=jnp.float32)
        mixed = jnp.where(inside, mixed, 0.0)
        for block in range(start // LANES, stop // LANES):
            piece = mixed[:, block * LANES - start : (block + 1) * LANES - start]
            blocks[block] = piece if blocks[block] is None else blocks[block] + piece
    return jnp.concatenate(blocks, axis=1).astype(jnp.bfloat16)


def attention_kernel(
    count_row,
    count_col,
    qw_hbm,
    kw_hbm,
    vw_hbm,
    qi_hbm,
    ki_hbm,
    pw_hbm,
    pb_ref,
    out_hbm,
    qw,
    kw,
    vw,
    pw,
    window_out,
    k_all,
    v_all,
    q_all,
    proj,
    load_sem,
    own_sem,
    q_own_sem,
    out_own_sem,
    k_send,
    k_recv,
    v_send,
    v_recv,
    q_send,
    q_recv,
    r_send,
    r_recv,
):
    count = count_row * count_col
    windows = qw.shape[0]
    owned = k_all.shape[2]
    features = qw.shape[2]
    me = lax.axis_index("row") * count_col + lax.axis_index("col")

    def offset(step):
        half = (step + 1) // 2
        return count // 2 + jnp.where(step % 2 == 1, half, -half)

    def peer_of(shift):
        return lax.rem(me + shift, count)

    def device(peer):
        return {"row": peer // count_col, "col": lax.rem(peer, count_col)}

    def tokens(peer):
        return pl.ds(pl.multiple_of(peer * owned, owned), owned)

    def copy_k(shift):
        peer = peer_of(shift)
        return pltpu.make_async_remote_copy(
            src_ref=ki_hbm.at[:, tokens(peer), :],
            dst_ref=k_all.at[me],
            send_sem=k_send.at[shift],
            recv_sem=k_recv.at[shift],
            device_id=device(peer),
            device_id_type=pl.DeviceIdType.MESH,
        )

    def copy_v(shift):
        peer = peer_of(shift)
        return pltpu.make_async_remote_copy(
            src_ref=window_out.at[:, tokens(peer), :],
            dst_ref=v_all.at[me],
            send_sem=v_send.at[shift],
            recv_sem=v_recv.at[shift],
            device_id=device(peer),
            device_id_type=pl.DeviceIdType.MESH,
        )

    def copy_q(window, shift):
        peer = peer_of(shift)
        return pltpu.make_async_remote_copy(
            src_ref=qi_hbm.at[window, tokens(peer), :],
            dst_ref=q_all.at[window, me],
            send_sem=q_send.at[window, shift],
            recv_sem=q_recv.at[window, shift],
            device_id=device(peer),
            device_id_type=pl.DeviceIdType.MESH,
        )

    def copy_r(window, shift):
        peer = peer_of(shift)
        return pltpu.make_async_remote_copy(
            src_ref=proj.at[window, tokens(peer), :],
            dst_ref=out_hbm.at[window, tokens(me), :],
            send_sem=r_send.at[window, shift],
            recv_sem=r_recv.at[window, shift],
            device_id=device(peer),
            device_id_type=pl.DeviceIdType.MESH,
        )

    def own_q(window):
        return pltpu.make_async_copy(
            qi_hbm.at[window, tokens(me), :], q_all.at[window, me], q_own_sem.at[window]
        )

    def own_r(window):
        return pltpu.make_async_copy(
            proj.at[window, tokens(me), :],
            out_hbm.at[window, tokens(me), :],
            out_own_sem.at[window],
        )

    loads = [
        pltpu.make_async_copy(source, target, load_sem.at[place])
        for place, (source, target) in enumerate(
            ((qw_hbm, qw), (kw_hbm, kw), (vw_hbm, vw), (pw_hbm, pw))
        )
    ]
    for load in loads:
        load.start()
    own_k = pltpu.make_async_copy(ki_hbm.at[:, tokens(me), :], k_all.at[me], own_sem.at[0])
    own_k.start()

    def each_shift(body):
        def step(index, carry):
            body(offset(index))
            return carry

        lax.fori_loop(0, count - 1, step, 0)

    def each_window(body):
        def step(index, carry):
            body(index)
            return carry

        lax.fori_loop(0, windows, step, 0)

    each_window(lambda window: own_q(window).start())

    barrier = pltpu.get_barrier_semaphore()

    def greet(shift):
        pl.semaphore_signal(
            barrier,
            inc=1,
            device_id=device(peer_of(shift)),
            device_id_type=pl.DeviceIdType.MESH,
        )

    each_shift(greet)
    pl.semaphore_wait(barrier, count - 1)
    each_shift(lambda shift: copy_k(shift).start())

    for load in loads:
        load.wait()

    def within(window):
        window_out[window] = attend_heads(
            qw[window],
            lambda start, stop: kw[window, :, start:stop],
            lambda start, stop: vw[window, :, start:stop],
            None,
        )

    each_window(within)
    own_v = pltpu.make_async_copy(
        window_out.at[:, tokens(me), :], v_all.at[me], own_sem.at[1]
    )
    own_v.start()
    each_shift(lambda shift: copy_v(shift).start())
    each_window(lambda window: each_shift(lambda shift: copy_q(window, shift).start()))

    own_k.wait()
    own_v.wait()
    each_shift(lambda shift: copy_k(shift).wait())
    each_shift(lambda shift: copy_v(shift).wait())

    key_rows = k_all.reshape(count * windows * owned, features)
    value_rows = v_all.reshape(count * windows * owned, features)
    query_rows = q_all.reshape(windows, count * owned, features)
    square = (count * owned, count * windows * owned)
    same = lax.rem(lax.broadcasted_iota(jnp.int32, square, 0), owned) == lax.rem(
        lax.broadcasted_iota(jnp.int32, square, 1), owned
    )

    def across(window):
        own_q(window).wait()
        each_shift(lambda shift: copy_q(window, shift).wait())
        mixed = attend_heads(
            query_rows[window],
            lambda start, stop: key_rows[:, start:stop],
            lambda start, stop: value_rows[:, start:stop],
            same,
        )
        rows = jnp.dot(mixed, pw[...], preferred_element_type=jnp.float32) + pb_ref[...]
        proj[window] = rows.astype(jnp.bfloat16)
        own_r(window).start()
        each_shift(lambda shift: copy_r(window, shift).start())

    each_window(across)

    def finish(window):
        own_r(window).wait()
        each_shift(lambda shift: copy_r(window, shift).wait())

    each_window(finish)


def attention_exchange(qw, kw, vw, qi, ki, proj_weight, proj_bias):
    windows, tokens_win, features = qw.shape
    count_row = lax.axis_size("row")
    count_col = lax.axis_size("col")
    count = count_row * count_col
    owned = tokens_win // count
    channels = proj_weight.shape[-1]
    whole = pl.BlockSpec(memory_space=pl.ANY)
    dma = pltpu.SemaphoreType.DMA
    return pl.pallas_call(
        functools.partial(attention_kernel, count_row, count_col),
        out_shape=jax.ShapeDtypeStruct((windows, tokens_win, channels), jnp.bfloat16),
        in_specs=[whole] * 6 + [pl.BlockSpec(memory_space=pltpu.VMEM)],
        out_specs=whole,
        scratch_shapes=[
            pltpu.VMEM(qw.shape, jnp.bfloat16),
            pltpu.VMEM(qw.shape, jnp.bfloat16),
            pltpu.VMEM(qw.shape, jnp.bfloat16),
            pltpu.VMEM(proj_weight.shape, jnp.bfloat16),
            pltpu.VMEM(qw.shape, jnp.bfloat16),
            pltpu.VMEM((count, windows, owned, features), jnp.bfloat16),
            pltpu.VMEM((count, windows, owned, features), jnp.bfloat16),
            pltpu.VMEM((windows, count, owned, features), jnp.bfloat16),
            pltpu.VMEM((windows, tokens_win, channels), jnp.bfloat16),
            dma((4,)),
            dma((2,)),
            dma((windows,)),
            dma((windows,)),
            dma((count,)),
            dma((count,)),
            dma((count,)),
            dma((count,)),
            dma((windows, count)),
            dma((windows, count)),
            dma((windows, count)),
            dma((windows, count)),
        ],
        compiler_params=pltpu.CompilerParams(
            collective_id=0, has_side_effects=True, vmem_limit_bytes=48 * 1024 * 1024
        ),
    )(qw, kw, vw, qi, ki, proj_weight, proj_bias.reshape(1, channels))


def convolutions(
    projected, rows_dev, cols_dev, first_kernel, first_bias, second_kernel, second_bias
):
    grouped = projected.reshape(rows_dev, cols_dev, TILE_ROWS, TILE_COLS, 2, 2, CHANNELS)
    shuffled = jnp.transpose(grouped, (0, 2, 4, 1, 3, 5, 6)).reshape(
        rows_dev * TILE_ROWS * 2, cols_dev * TILE_COLS * 2, CHANNELS
    )
    activated = jax.nn.gelu(convolve(shuffled, first_kernel, first_bias)).astype(jnp.bfloat16)
    return convolve(activated, second_kernel, second_bias).astype(jnp.bfloat16)


def shards(
    query_window,
    key_window,
    value_window,
    query_index,
    key_index,
    proj_weight,
    proj_bias,
    first_kernel,
    first_bias,
    second_kernel,
    second_bias,
):
    rows_dev, cols_dev, tokens_win, features = query_window.shape
    flat = (rows_dev * cols_dev, tokens_win, features)
    owners = lax.axis_size("row") * lax.axis_size("col")
    if tokens_win % (owners * 8) == 0 and features % LANES == 0:
        projected = attention_exchange(
            query_window.reshape(flat),
            key_window.reshape(flat),
            value_window.reshape(flat),
            query_index.reshape(flat),
            key_index.reshape(flat),
            proj_weight,
            proj_bias,
        )
        return convolutions(
            projected, rows_dev, cols_dev, first_kernel, first_bias, second_kernel, second_bias
        )
    layout = (rows_dev * cols_dev, tokens_win, HEADS, HEAD_DIM)
    window_out = window_attend(
        query_window.reshape(layout), key_window.reshape(layout), value_window.reshape(layout)
    ).reshape(query_window.shape)
    count_row = lax.axis_size("row")
    count_col = lax.axis_size("col")
    owned_tokens = tokens_win // (count_row * count_col)
    moved = (
        lax.all_to_all(query_index, ("row", "col"), split_axis=2, concat_axis=0, tiled=True),
        lax.all_to_all(key_index, ("row", "col"), split_axis=2, concat_axis=0, tiled=True),
        lax.all_to_all(window_out, ("row", "col"), split_axis=2, concat_axis=0, tiled=True),
    )
    owner_shape = moved[0].shape
    across = (-1, owned_tokens, HEADS, HEAD_DIM)
    index_out = index_attend(
        moved[0].reshape(across), moved[1].reshape(across), moved[2].reshape(across)
    )
    index_rows = index_out.reshape(-1, features)
    owner_rows = (
        jnp.dot(index_rows, proj_weight, preferred_element_type=jnp.float32) + proj_bias
    ).astype(jnp.bfloat16)
    last = owner_rows.shape[-1]
    shaped = owner_rows.reshape(tuple(owner_shape[:-1]) + (last,))
    returned = lax.all_to_all(shaped, ("row", "col"), split_axis=0, concat_axis=2, tiled=True)
    projected = returned.reshape(rows_dev * cols_dev * tokens_win, last)
    return convolutions(
        projected, rows_dev, cols_dev, first_kernel, first_bias, second_kernel, second_bias
    )


def solution(mesh):
    in_specs = (
        P(("grp", "row"), "col", None, None),
        P(("grp", "row"), "col", None, None),
        P(("grp", "row"), "col", None, None),
        P(("grp", "row"), "col", None, None),
        P(("grp", "row"), "col", None, None),
        P(),
        P(),
        P(),
        P(),
        P(),
        P(),
    )
    out_specs = P(("grp", "row"), "col", None)
    return jax.shard_map(shards, mesh=mesh, in_specs=in_specs, out_specs=out_specs, check_vma=False)
```

```python
import functools
import math

import jax
import jax.numpy as jnp
from jax import lax
from jax.experimental import pallas as pl
from jax.experimental.pallas import tpu as pltpu
from jax.sharding import PartitionSpec as P

HEADS = 8
HEAD_DIM = 160
CHANNELS = 256
TILE_ROWS = 8
TILE_COLS = 16
LANES = 128


def extended(value, sides, width):
    for axis, dim in sides:
        size, length = (lax.axis_size(axis), value.shape[dim])
        up = [(i, (i + 1) % size) for i in range(size - 1)]
        down = [(j, i) for i, j in up]
        last = lax.slice_in_dim(value, length - width, length, axis=dim)
        first = lax.slice_in_dim(value, 0, width, axis=dim)
        before = lax.ppermute(last, axis, up)
        after = lax.ppermute(first, axis, down)
        value = jnp.concatenate([before, value, after], axis=dim)
    return value


def softmax_rows(scores):
    highest = jnp.max(scores, axis=-1, keepdims=True)
    raised = jnp.exp(scores - highest)
    return (raised / jnp.sum(raised, axis=-1, keepdims=True)).astype(jnp.bfloat16)


def window_attend(queries, key_rows, values):
    scores = jnp.einsum(
        "blhd,bmhd->bhlm", queries, key_rows, preferred_element_type=jnp.float32
    ) / math.sqrt(HEAD_DIM)
    weights = softmax_rows(scores)
    return jnp.einsum(
        "bhlm,bmhd->blhd", weights, values, preferred_element_type=jnp.float32
    ).astype(jnp.bfloat16)


def index_attend(queries, key_rows, values):
    scores = jnp.einsum(
        "lbhd,mbhd->bhlm", queries, key_rows, preferred_element_type=jnp.float32
    ) / math.sqrt(HEAD_DIM)
    weights = softmax_rows(scores)
    return jnp.einsum(
        "bhlm,mbhd->lbhd", weights, values, preferred_element_type=jnp.float32
    ).astype(jnp.bfloat16)


def convolve(image, kernel, bias):
    height, breadth, depth = image.shape
    padded = extended(image, (("row", 0), ("col", 1)), 1)
    total = jnp.zeros((height * breadth, kernel.shape[-1]), jnp.float32)
    for row_shift in range(3):
        for col_shift in range(3):
            cells = padded[row_shift : row_shift + height, col_shift : col_shift + breadth].reshape(
                -1, depth
            )
            total = total + jnp.dot(
                cells, kernel[row_shift, col_shift], preferred_element_type=jnp.float32
            )
    return (total + bias).reshape(height, breadth, -1)


def attend_heads(queries, key_part, value_part, same):
    rows, features = queries.shape
    head_dim = features // HEADS
    factor = math.log2(math.e) / math.sqrt(head_dim)
    blocks = [None] * (features // LANES)
    for head in range(HEADS):
        low, high = (head * head_dim, (head + 1) * head_dim)
        start, stop = (low // LANES * LANES, -(-high // LANES) * LANES)
        lane = lax.broadcasted_iota(jnp.int32, (rows, stop - start), 1) + start
        inside = (lane >= low) & (lane < high)
        part = queries[:, start:stop]
        part = jnp.where(inside, part, jnp.zeros_like(part))
        scores = lax.dot_general(
            part,
            key_part(start, stop),
            (((1,), (1,)), ((), ())),
            preferred_element_type=jnp.float32,
        )
        if same is not None:
            scores = jnp.where(same, scores, -1e30)
        highest = jnp.max(scores, axis=-1, keepdims=True)
        raised = jnp.exp2((scores - highest) * factor)
        weights = (raised * (1.0 / jnp.sum(raised, axis=-1, keepdims=True))).astype(jnp.bfloat16)
        mixed = jnp.dot(weights, value_part(start, stop), preferred_element_type=jnp.float32)
        mixed = jnp.where(inside, mixed, 0.0)
        for block in range(start // LANES, stop // LANES):
            piece = mixed[:, block * LANES - start : (block + 1) * LANES - start]
            blocks[block] = piece if blocks[block] is None else blocks[block] + piece
    return jnp.concatenate(blocks, axis=1).astype(jnp.bfloat16)


def attention_kernel(
    count_row,
    count_col,
    qw_hbm,
    kw_hbm,
    vw_hbm,
    qi_hbm,
    ki_hbm,
    pw_hbm,
    fk_hbm,
    sk_hbm,
    pb_ref,
    fb_ref,
    sb_ref,
    out_ref,
    qw,
    kw,
    vw,
    pw,
    window_out,
    k_all,
    v_all,
    q_all,
    proj,
    field,
    fk,
    sk,
    halo_up,
    halo_down,
    side_right,
    side_left,
    shuffled,
    activated,
    load_sem,
    own_sem,
    q_own_sem,
    out_own_sem,
    k_send,
    k_recv,
    v_send,
    v_recv,
    q_send,
    q_recv,
    r_send,
    r_recv,
    edge_send,
    edge_recv,
    side_send,
    side_recv,
):
    count = count_row * count_col
    windows = qw.shape[0]
    owned = k_all.shape[2]
    features = qw.shape[2]
    me = lax.axis_index("row") * count_col + lax.axis_index("col")

    def offset(step):
        half = (step + 1) // 2
        return count // 2 + jnp.where(step % 2 == 1, half, -half)

    def peer_of(shift):
        return lax.rem(me + shift, count)

    def device(peer):
        return {"row": peer // count_col, "col": lax.rem(peer, count_col)}

    def tokens(peer):
        return pl.ds(pl.multiple_of(peer * owned, owned), owned)

    def copy_k(shift):
        peer = peer_of(shift)
        return pltpu.make_async_remote_copy(
            src_ref=ki_hbm.at[:, tokens(peer), :],
            dst_ref=k_all.at[me],
            send_sem=k_send.at[shift],
            recv_sem=k_recv.at[shift],
            device_id=device(peer),
            device_id_type=pl.DeviceIdType.MESH,
        )

    def copy_v(shift):
        peer = peer_of(shift)
        return pltpu.make_async_remote_copy(
            src_ref=window_out.at[:, tokens(peer), :],
            dst_ref=v_all.at[me],
            send_sem=v_send.at[shift],
            recv_sem=v_recv.at[shift],
            device_id=device(peer),
            device_id_type=pl.DeviceIdType.MESH,
        )

    def copy_q(window, shift):
        peer = peer_of(shift)
        return pltpu.make_async_remote_copy(
            src_ref=qi_hbm.at[window, tokens(peer), :],
            dst_ref=q_all.at[window, me],
            send_sem=q_send.at[window, shift],
            recv_sem=q_recv.at[window, shift],
            device_id=device(peer),
            device_id_type=pl.DeviceIdType.MESH,
        )

    def copy_r(window, shift):
        peer = peer_of(shift)
        return pltpu.make_async_remote_copy(
            src_ref=proj.at[window, tokens(peer), :],
            dst_ref=field.at[window, tokens(me), :],
            send_sem=r_send.at[window, shift],
            recv_sem=r_recv.at[window, shift],
            device_id=device(peer),
            device_id_type=pl.DeviceIdType.MESH,
        )

    def own_q(window):
        return pltpu.make_async_copy(
            qi_hbm.at[window, tokens(me), :], q_all.at[window, me], q_own_sem.at[window]
        )

    def own_r(window):
        return pltpu.make_async_copy(
            proj.at[window, tokens(me), :],
            field.at[window, tokens(me), :],
            out_own_sem.at[window],
        )

    loads = [
        pltpu.make_async_copy(source, target, load_sem.at[place])
        for place, (source, target) in enumerate(
            (
                (qw_hbm, qw),
                (kw_hbm, kw),
                (vw_hbm, vw),
                (pw_hbm, pw),
                (fk_hbm, fk),
                (sk_hbm, sk),
            )
        )
    ]
    for load in loads:
        load.start()
    own_k = pltpu.make_async_copy(ki_hbm.at[:, tokens(me), :], k_all.at[me], own_sem.at[0])
    own_k.start()

    def each_shift(body):
        def step(index, carry):
            body(offset(index))
            return carry

        lax.fori_loop(0, count - 1, step, 0)

    def each_window(body):
        def step(index, carry):
            body(index)
            return carry

        lax.fori_loop(0, windows, step, 0)

    each_window(lambda window: own_q(window).start())
    for halo in (halo_up, halo_down, side_right, side_left):
        halo[...] = jnp.zeros_like(halo)

    barrier = pltpu.get_barrier_semaphore()

    def greet(shift):
        pl.semaphore_signal(
            barrier,
            inc=1,
            device_id=device(peer_of(shift)),
            device_id_type=pl.DeviceIdType.MESH,
        )

    each_shift(greet)
    pl.semaphore_wait(barrier, count - 1)
    each_shift(lambda shift: copy_k(shift).start())

    for load in loads:
        load.wait()

    def within(window):
        window_out[window] = attend_heads(
            qw[window],
            lambda start, stop: kw[window, :, start:stop],
            lambda start, stop: vw[window, :, start:stop],
            None,
        )

    each_window(within)
    own_v = pltpu.make_async_copy(
        window_out.at[:, tokens(me), :], v_all.at[me], own_sem.at[1]
    )
    own_v.start()
    each_shift(lambda shift: copy_v(shift).start())
    each_window(lambda window: each_shift(lambda shift: copy_q(window, shift).start()))

    own_k.wait()
    own_v.wait()
    each_shift(lambda shift: copy_k(shift).wait())
    each_shift(lambda shift: copy_v(shift).wait())

    key_rows = k_all.reshape(count * windows * owned, features)
    value_rows = v_all.reshape(count * windows * owned, features)
    query_rows = q_all.reshape(windows, count * owned, features)
    square = (count * owned, count * windows * owned)
    same = lax.rem(lax.broadcasted_iota(jnp.int32, square, 0), owned) == lax.rem(
        lax.broadcasted_iota(jnp.int32, square, 1), owned
    )

    def across(window):
        own_q(window).wait()
        each_shift(lambda shift: copy_q(window, shift).wait())
        mixed = attend_heads(
            query_rows[window],
            lambda start, stop: key_rows[:, start:stop],
            lambda start, stop: value_rows[:, start:stop],
            same,
        )
        rows = jnp.dot(mixed, pw[...], preferred_element_type=jnp.float32) + pb_ref[...]
        proj[window] = rows.astype(jnp.bfloat16)
        own_r(window).start()
        each_shift(lambda shift: copy_r(window, shift).start())

    each_window(across)

    my_row, my_col = (lax.axis_index("row"), lax.axis_index("col"))
    has_up, has_down = (my_row > 0, my_row < count_row - 1)
    has_left, has_right = (my_col > 0, my_col < count_col - 1)
    tokens_win = field.shape[1]
    tile = TILE_COLS

    def copy_to(source, target, sems, step_row, step_col):
        return pltpu.make_async_remote_copy(
            src_ref=source,
            dst_ref=target,
            send_sem=sems[0],
            recv_sem=sems[1],
            device_id={"row": my_row + step_row, "col": my_col + step_col},
            device_id_type=pl.DeviceIdType.MESH,
        )

    def edge(window, down):
        source = pl.ds(tokens_win - tile if down else 0, tile)
        target = halo_up if down else halo_down
        place = 0 if down else 1
        return copy_to(
            field.at[window, source, :],
            target.at[window],
            (edge_send.at[place, window], edge_recv.at[place, window]),
            1 if down else -1,
            0,
        )

    def side(right, step_row):
        window = windows - 1 if right else 0
        target = side_left if right else side_right
        place = (0 if right else 3) + step_row + 1
        if step_row == 0:
            source, rows = (pl.ds(0, tokens_win), pl.ds(tile, tokens_win))
        elif step_row > 0:
            source, rows = (pl.ds(tokens_win - tile, tile), pl.ds(0, tile))
        else:
            source, rows = (pl.ds(0, tile), pl.ds(tokens_win + tile, tile))
        return copy_to(
            field.at[window, source, :],
            target.at[rows, :],
            (side_send.at[place], side_recv.at[place]),
            step_row,
            1 if right else -1,
        )

    row_ways = ((0, None, None), (1, has_down, has_up), (-1, has_up, has_down))

    def send_sides(right):
        there = has_right if right else has_left
        for step_row, goes, _ in row_ways:

            @pl.when(there if goes is None else there & goes)
            def _():
                side(right, step_row).start()

    def finish(window):
        own_r(window).wait()
        each_shift(lambda shift: copy_r(window, shift).wait())
        for down, goes in ((True, has_down), (False, has_up)):

            @pl.when(goes)
            def _():
                edge(window, down).start()

    finish(0)
    send_sides(False)

    def later(window, carry):
        finish(window)
        return carry

    lax.fori_loop(1, windows, later, 0)
    send_sides(True)

    depth = fk.shape[-1]
    width = (windows + 1) * tile
    token_rows = tokens_win // tile
    total = shuffled.shape[1]

    for window in range(windows):
        for line in range(token_rows):
            start = tile + (line + 1) * width + window * tile
            for parity in range(2):
                shuffled[parity, start : start + tile, depth : 3 * depth] = field[
                    window,
                    line * tile : (line + 1) * tile,
                    parity * 2 * depth : (parity + 1) * 2 * depth,
                ]

    for window in range(windows):
        for down, goes, comes in ((True, has_down, has_up), (False, has_up, has_down)):

            @pl.when(goes)
            def _():
                edge(window, down).wait_send()

            @pl.when(comes)
            def _():
                edge(window, down).wait_recv()

    for right in (True, False):
        there, here = (has_right, has_left) if right else (has_left, has_right)
        for step_row, goes, comes in row_ways:

            @pl.when(there if goes is None else there & goes)
            def _():
                side(right, step_row).wait_send()

            @pl.when(here if comes is None else here & comes)
            def _():
                side(right, step_row).wait_recv()

    for parity in range(2):
        lanes = slice(parity * 2 * depth, (parity + 1) * 2 * depth)
        for window in range(windows):
            for source, line in ((halo_up, 0), (halo_down, token_rows + 1)):
                start = tile + line * width + window * tile
                shuffled[parity, start : start + tile, depth : 3 * depth] = source[
                    window, :, lanes
                ]
        first = lax.broadcasted_iota(jnp.int32, (tile, 2 * depth), 0) < tile // 2
        shuffled[parity, 0:tile, depth : 3 * depth] = side_left[0:tile, lanes]
        for line in range(token_rows + 2):
            start = tile + line * width + windows * tile
            block = side_right[line * tile : (line + 1) * tile, lanes]
            if line < token_rows + 1:
                after = side_left[(line + 1) * tile : (line + 2) * tile, lanes]
                block = jnp.where(first, block, after)
            shuffled[parity, start : start + tile, depth : 3 * depth] = block
        odd = shuffled[parity, :, 2 * depth : 3 * depth].astype(jnp.float32)
        shuffled[parity, :, 0:depth] = pltpu.roll(odd, 1, 0).astype(jnp.bfloat16)
        even = shuffled[parity, :, depth : 2 * depth].astype(jnp.float32)
        shuffled[parity, :, 3 * depth :] = pltpu.roll(even, total - 1, 0).astype(jnp.bfloat16)

    def convolve_rows(source, weights, row_parity, col_parity, start, size):
        if row_parity == 0:
            taps = ((1, -width), (0, 0), (1, 0))
        else:
            taps = ((0, 0), (1, 0), (0, width))
        result = None
        for tap, (parity, shift) in enumerate(taps):
            cells = source[
                parity,
                start + shift : start + shift + size,
                col_parity * depth : (col_parity + 3) * depth,
            ]
            part = jnp.dot(cells, weights[tap], preferred_element_type=jnp.float32)
            result = part if result is None else result + part
        return result

    size = total - width
    main = windows * tile
    right_stop = jnp.where(has_right, main + tile // 2, main)
    left_start = jnp.where(has_left, main + tile // 2, width)
    line_start = jnp.where(has_up, 0, 1)
    line_stop = jnp.where(has_down, token_rows + 2, token_rows + 1)
    for parity in range(2):
        start = width if parity == 0 else 0
        place = lax.broadcasted_iota(jnp.int32, (size, depth), 0) + start
        column = lax.rem(place + (width - tile), width)
        line = lax.div(place + (width - tile) + tile // 2, width) - 1
        valid = (column < right_stop) | (column >= left_start)
        valid = valid & ((line < line_stop) if parity == 0 else (line >= line_start))
        for other in range(2):
            value = convolve_rows(shuffled, fk, parity, other, start, size) + fb_ref[...]
            value = jnp.where(valid, jax.nn.gelu(value), 0.0)
            rows = slice(start, start + size)
            activated[parity, rows, (other + 1) * depth : (other + 2) * depth] = value.astype(
                jnp.bfloat16
            )
            if other == 1:
                moved = pltpu.roll(value, 1, 0)
                activated[parity, rows, 0:depth] = moved.astype(jnp.bfloat16)
            else:
                moved = pltpu.roll(value, size - 1, 0)
                activated[parity, rows, 3 * depth :] = moved.astype(jnp.bfloat16)

    for parity in range(2):
        for other in range(2):
            value = convolve_rows(
                activated, sk, parity, other, tile + width, token_rows * width
            )
            value = (value + sb_ref[...]).astype(jnp.bfloat16)
            for line in range(token_rows):
                out_ref[2 * line + parity, :, other * depth : (other + 1) * depth] = value[
                    line * width : line * width + windows * tile
                ]


def fused(qw, kw, vw, qi, ki, proj_weight, proj_bias, first_kernel, first_bias, second_kernel, second_bias):
    windows, tokens_win, features = qw.shape
    count_row = lax.axis_size("row")
    count_col = lax.axis_size("col")
    count = count_row * count_col
    owned = tokens_win // count
    channels = proj_weight.shape[-1]
    depth = first_kernel.shape[-1]
    taps = (first_kernel.shape[0], first_kernel.shape[1] * first_kernel.shape[2], depth)
    token_rows = tokens_win // TILE_COLS
    width = (windows + 1) * TILE_COLS
    planes = (2, TILE_COLS + (token_rows + 2) * width, 4 * depth)
    whole = pl.BlockSpec(memory_space=pl.ANY)
    held = pl.BlockSpec(memory_space=pltpu.VMEM)
    dma = pltpu.SemaphoreType.DMA
    return pl.pallas_call(
        functools.partial(attention_kernel, count_row, count_col),
        out_shape=jax.ShapeDtypeStruct(
            (2 * token_rows, windows * TILE_COLS, 2 * depth), jnp.bfloat16
        ),
        in_specs=[whole] * 8 + [held] * 3,
        out_specs=held,
        scratch_shapes=[
            pltpu.VMEM(qw.shape, jnp.bfloat16),
            pltpu.VMEM(qw.shape, jnp.bfloat16),
            pltpu.VMEM(qw.shape, jnp.bfloat16),
            pltpu.VMEM(proj_weight.shape, jnp.bfloat16),
            pltpu.VMEM(qw.shape, jnp.bfloat16),
            pltpu.VMEM((count, windows, owned, features), jnp.bfloat16),
            pltpu.VMEM((count, windows, owned, features), jnp.bfloat16),
            pltpu.VMEM((windows, count, owned, features), jnp.bfloat16),
            pltpu.VMEM((windows, tokens_win, channels), jnp.bfloat16),
            pltpu.VMEM((windows, tokens_win, channels), jnp.bfloat16),
            pltpu.VMEM(taps, jnp.bfloat16),
            pltpu.VMEM(taps, jnp.bfloat16),
            pltpu.VMEM((windows, TILE_COLS, channels), jnp.bfloat16),
            pltpu.VMEM((windows, TILE_COLS, channels), jnp.bfloat16),
            pltpu.VMEM((tokens_win + 2 * TILE_COLS, channels), jnp.bfloat16),
            pltpu.VMEM((tokens_win + 2 * TILE_COLS, channels), jnp.bfloat16),
            pltpu.VMEM(planes, jnp.bfloat16),
            pltpu.VMEM(planes, jnp.bfloat16),
            dma((6,)),
            dma((2,)),
            dma((windows,)),
            dma((windows,)),
            dma((count,)),
            dma((count,)),
            dma((count,)),
            dma((count,)),
            dma((windows, count)),
            dma((windows, count)),
            dma((windows, count)),
            dma((windows, count)),
            dma((2, windows)),
            dma((2, windows)),
            dma((6,)),
            dma((6,)),
        ],
        compiler_params=pltpu.CompilerParams(
            collective_id=0, has_side_effects=True, vmem_limit_bytes=62 * 1024 * 1024
        ),
    )(
        qw,
        kw,
        vw,
        qi,
        ki,
        proj_weight,
        first_kernel.reshape(taps),
        second_kernel.reshape(taps),
        proj_bias.reshape(1, channels),
        first_bias.reshape(1, depth),
        second_bias.reshape(1, depth),
    )


def convolutions(
    projected, rows_dev, cols_dev, first_kernel, first_bias, second_kernel, second_bias
):
    grouped = projected.reshape(rows_dev, cols_dev, TILE_ROWS, TILE_COLS, 2, 2, CHANNELS)
    shuffled = jnp.transpose(grouped, (0, 2, 4, 1, 3, 5, 6)).reshape(
        rows_dev * TILE_ROWS * 2, cols_dev * TILE_COLS * 2, CHANNELS
    )
    activated = jax.nn.gelu(convolve(shuffled, first_kernel, first_bias)).astype(jnp.bfloat16)
    return convolve(activated, second_kernel, second_bias).astype(jnp.bfloat16)


def shards(
    query_window,
    key_window,
    value_window,
    query_index,
    key_index,
    proj_weight,
    proj_bias,
    first_kernel,
    first_bias,
    second_kernel,
    second_bias,
):
    rows_dev, cols_dev, tokens_win, features = query_window.shape
    flat = (rows_dev * cols_dev, tokens_win, features)
    owners = lax.axis_size("row") * lax.axis_size("col")
    if rows_dev == 1 and tokens_win % (owners * 8) == 0 and features % LANES == 0:
        fine = fused(
            query_window.reshape(flat),
            key_window.reshape(flat),
            value_window.reshape(flat),
            query_index.reshape(flat),
            key_index.reshape(flat),
            proj_weight,
            proj_bias,
            first_kernel,
            first_bias,
            second_kernel,
            second_bias,
        )
        return fine.reshape(fine.shape[0], 2 * fine.shape[1], -1)
    layout = (rows_dev * cols_dev, tokens_win, HEADS, HEAD_DIM)
    window_out = window_attend(
        query_window.reshape(layout), key_window.reshape(layout), value_window.reshape(layout)
    ).reshape(query_window.shape)
    count_row = lax.axis_size("row")
    count_col = lax.axis_size("col")
    owned_tokens = tokens_win // (count_row * count_col)
    moved = (
        lax.all_to_all(query_index, ("row", "col"), split_axis=2, concat_axis=0, tiled=True),
        lax.all_to_all(key_index, ("row", "col"), split_axis=2, concat_axis=0, tiled=True),
        lax.all_to_all(window_out, ("row", "col"), split_axis=2, concat_axis=0, tiled=True),
    )
    owner_shape = moved[0].shape
    across = (-1, owned_tokens, HEADS, HEAD_DIM)
    index_out = index_attend(
        moved[0].reshape(across), moved[1].reshape(across), moved[2].reshape(across)
    )
    index_rows = index_out.reshape(-1, features)
    owner_rows = (
        jnp.dot(index_rows, proj_weight, preferred_element_type=jnp.float32) + proj_bias
    ).astype(jnp.bfloat16)
    last = owner_rows.shape[-1]
    shaped = owner_rows.reshape(tuple(owner_shape[:-1]) + (last,))
    returned = lax.all_to_all(shaped, ("row", "col"), split_axis=0, concat_axis=2, tiled=True)
    projected = returned.reshape(rows_dev * cols_dev * tokens_win, last)
    return convolutions(
        projected, rows_dev, cols_dev, first_kernel, first_bias, second_kernel, second_bias
    )


def solution(mesh):
    in_specs = (
        P(("grp", "row"), "col", None, None),
        P(("grp", "row"), "col", None, None),
        P(("grp", "row"), "col", None, None),
        P(("grp", "row"), "col", None, None),
        P(("grp", "row"), "col", None, None),
        P(),
        P(),
        P(),
        P(),
        P(),
        P(),
    )
    out_specs = P(("grp", "row"), "col", None)
    return jax.shard_map(shards, mesh=mesh, in_specs=in_specs, out_specs=out_specs, check_vma=False)
```

```python
import functools
import math

import jax
import jax.numpy as jnp
from jax import lax
from jax.experimental import pallas as pl
from jax.experimental.pallas import tpu as pltpu
from jax.sharding import PartitionSpec as P

HEADS = 8
HEAD_DIM = 160
CHANNELS = 256
TILE_ROWS = 8
TILE_COLS = 16
LANES = 128


def extended(value, sides, width):
    for axis, dim in sides:
        size, length = (lax.axis_size(axis), value.shape[dim])
        up = [(i, (i + 1) % size) for i in range(size - 1)]
        down = [(j, i) for i, j in up]
        last = lax.slice_in_dim(value, length - width, length, axis=dim)
        first = lax.slice_in_dim(value, 0, width, axis=dim)
        before = lax.ppermute(last, axis, up)
        after = lax.ppermute(first, axis, down)
        value = jnp.concatenate([before, value, after], axis=dim)
    return value


def softmax_rows(scores):
    highest = jnp.max(scores, axis=-1, keepdims=True)
    raised = jnp.exp(scores - highest)
    return (raised / jnp.sum(raised, axis=-1, keepdims=True)).astype(jnp.bfloat16)


def window_attend(queries, key_rows, values):
    scores = jnp.einsum(
        "blhd,bmhd->bhlm", queries, key_rows, preferred_element_type=jnp.float32
    ) / math.sqrt(HEAD_DIM)
    weights = softmax_rows(scores)
    return jnp.einsum(
        "bhlm,bmhd->blhd", weights, values, preferred_element_type=jnp.float32
    ).astype(jnp.bfloat16)


def index_attend(queries, key_rows, values):
    scores = jnp.einsum(
        "lbhd,mbhd->bhlm", queries, key_rows, preferred_element_type=jnp.float32
    ) / math.sqrt(HEAD_DIM)
    weights = softmax_rows(scores)
    return jnp.einsum(
        "bhlm,mbhd->lbhd", weights, values, preferred_element_type=jnp.float32
    ).astype(jnp.bfloat16)


def convolve(image, kernel, bias):
    height, breadth, depth = image.shape
    padded = extended(image, (("row", 0), ("col", 1)), 1)
    total = jnp.zeros((height * breadth, kernel.shape[-1]), jnp.float32)
    for row_shift in range(3):
        for col_shift in range(3):
            cells = padded[row_shift : row_shift + height, col_shift : col_shift + breadth].reshape(
                -1, depth
            )
            total = total + jnp.dot(
                cells, kernel[row_shift, col_shift], preferred_element_type=jnp.float32
            )
    return (total + bias).reshape(height, breadth, -1)


def attend_heads(queries, key_part, value_part, same):
    rows, features = queries.shape
    head_dim = features // HEADS
    factor = math.log2(math.e) / math.sqrt(head_dim)
    blocks = [None] * (features // LANES)
    for head in range(HEADS):
        low, high = (head * head_dim, (head + 1) * head_dim)
        start, stop = (low // LANES * LANES, -(-high // LANES) * LANES)
        lane = lax.broadcasted_iota(jnp.int32, (rows, stop - start), 1) + start
        inside = (lane >= low) & (lane < high)
        part = queries[:, start:stop]
        part = jnp.where(inside, part, jnp.zeros_like(part))
        scores = lax.dot_general(
            part,
            key_part(start, stop),
            (((1,), (1,)), ((), ())),
            preferred_element_type=jnp.float32,
        )
        if same is not None:
            scores = jnp.where(same, scores, -1e30)
        highest = jnp.max(scores, axis=-1, keepdims=True)
        raised = jnp.exp2((scores - highest) * factor)
        weights = (raised * (1.0 / jnp.sum(raised, axis=-1, keepdims=True))).astype(jnp.bfloat16)
        mixed = jnp.dot(weights, value_part(start, stop), preferred_element_type=jnp.float32)
        mixed = jnp.where(inside, mixed, 0.0)
        for block in range(start // LANES, stop // LANES):
            piece = mixed[:, block * LANES - start : (block + 1) * LANES - start]
            blocks[block] = piece if blocks[block] is None else blocks[block] + piece
    return jnp.concatenate(blocks, axis=1).astype(jnp.bfloat16)


def attention_kernel(
    count_row,
    count_col,
    qw_hbm,
    kw_hbm,
    vw_hbm,
    qi_hbm,
    ki_hbm,
    pw_hbm,
    fk_hbm,
    sk_hbm,
    pb_ref,
    fb_ref,
    sb_ref,
    out_ref,
    qw,
    kw,
    vw,
    pw,
    window_out,
    k_all,
    v_all,
    q_all,
    proj,
    field,
    fk,
    sk,
    halo_up,
    halo_down,
    side_right,
    side_left,
    shuffled,
    activated,
    load_sem,
    own_sem,
    q_own_sem,
    out_own_sem,
    k_send,
    k_recv,
    v_send,
    v_recv,
    q_send,
    q_recv,
    r_send,
    r_recv,
    edge_send,
    edge_recv,
    side_send,
    side_recv,
):
    count = count_row * count_col
    windows = qw.shape[0]
    owned = k_all.shape[2]
    features = qw.shape[2]
    me = lax.axis_index("row") * count_col + lax.axis_index("col")

    my_row, my_col = (lax.axis_index("row"), lax.axis_index("col"))
    has_up, has_down = (my_row > 0, my_row < count_row - 1)
    has_left, has_right = (my_col > 0, my_col < count_col - 1)

    def ordered(step):
        return jnp.where(has_left, step, windows - 1 - step)

    def offset(step):
        half = (step + 1) // 2
        return count // 2 + jnp.where(step % 2 == 1, half, -half)

    def peer_of(shift):
        return lax.rem(me + shift, count)

    def device(peer):
        return {"row": peer // count_col, "col": lax.rem(peer, count_col)}

    def tokens(peer):
        return pl.ds(pl.multiple_of(peer * owned, owned), owned)

    def copy_k(shift):
        peer = peer_of(shift)
        return pltpu.make_async_remote_copy(
            src_ref=ki_hbm.at[:, tokens(peer), :],
            dst_ref=k_all.at[me],
            send_sem=k_send.at[shift],
            recv_sem=k_recv.at[shift],
            device_id=device(peer),
            device_id_type=pl.DeviceIdType.MESH,
        )

    def copy_v(shift):
        peer = peer_of(shift)
        return pltpu.make_async_remote_copy(
            src_ref=window_out.at[:, tokens(peer), :],
            dst_ref=v_all.at[me],
            send_sem=v_send.at[shift],
            recv_sem=v_recv.at[shift],
            device_id=device(peer),
            device_id_type=pl.DeviceIdType.MESH,
        )

    def copy_q(window, shift):
        peer = peer_of(shift)
        return pltpu.make_async_remote_copy(
            src_ref=qi_hbm.at[ordered(window), tokens(peer), :],
            dst_ref=q_all.at[window, me],
            send_sem=q_send.at[window, shift],
            recv_sem=q_recv.at[window, shift],
            device_id=device(peer),
            device_id_type=pl.DeviceIdType.MESH,
        )

    def copy_r(window, shift):
        peer = peer_of(shift)
        return pltpu.make_async_remote_copy(
            src_ref=proj.at[window, tokens(peer), :],
            dst_ref=field.at[window, tokens(me), :],
            send_sem=r_send.at[window, shift],
            recv_sem=r_recv.at[window, shift],
            device_id=device(peer),
            device_id_type=pl.DeviceIdType.MESH,
        )

    def own_q(window):
        return pltpu.make_async_copy(
            qi_hbm.at[ordered(window), tokens(me), :], q_all.at[window, me], q_own_sem.at[window]
        )

    def own_r(window):
        return pltpu.make_async_copy(
            proj.at[window, tokens(me), :],
            field.at[window, tokens(me), :],
            out_own_sem.at[window],
        )

    loads = [
        pltpu.make_async_copy(source, target, load_sem.at[place])
        for place, (source, target) in enumerate(
            (
                (qw_hbm, qw),
                (kw_hbm, kw),
                (vw_hbm, vw),
                (pw_hbm, pw),
                (fk_hbm, fk),
                (sk_hbm, sk),
            )
        )
    ]
    for load in loads:
        load.start()
    own_k = pltpu.make_async_copy(ki_hbm.at[:, tokens(me), :], k_all.at[me], own_sem.at[0])
    own_k.start()

    def each_shift(body):
        def step(index, carry):
            body(offset(index))
            return carry

        lax.fori_loop(0, count - 1, step, 0)

    def each_window(body):
        def step(index, carry):
            body(index)
            return carry

        lax.fori_loop(0, windows, step, 0)

    each_window(lambda window: own_q(window).start())
    for halo in (halo_up, halo_down, side_right, side_left):
        halo[...] = jnp.zeros_like(halo)
    for outer in (0, windows + 1):
        for parity in range(2):
            activated[parity, outer] = jnp.zeros_like(activated[parity, outer])

    barrier = pltpu.get_barrier_semaphore()

    def greet(shift):
        pl.semaphore_signal(
            barrier,
            inc=1,
            device_id=device(peer_of(shift)),
            device_id_type=pl.DeviceIdType.MESH,
        )

    each_shift(greet)
    pl.semaphore_wait(barrier, count - 1)
    each_shift(lambda shift: copy_k(shift).start())

    for load in loads:
        load.wait()

    def within(window):
        window_out[window] = attend_heads(
            qw[window],
            lambda start, stop: kw[window, :, start:stop],
            lambda start, stop: vw[window, :, start:stop],
            None,
        )

    each_window(within)
    own_v = pltpu.make_async_copy(
        window_out.at[:, tokens(me), :], v_all.at[me], own_sem.at[1]
    )
    own_v.start()
    each_shift(lambda shift: copy_v(shift).start())
    each_window(lambda window: each_shift(lambda shift: copy_q(window, shift).start()))

    own_k.wait()
    own_v.wait()
    each_shift(lambda shift: copy_k(shift).wait())
    each_shift(lambda shift: copy_v(shift).wait())

    key_rows = k_all.reshape(count * windows * owned, features)
    value_rows = v_all.reshape(count * windows * owned, features)
    query_rows = q_all.reshape(windows, count * owned, features)
    square = (count * owned, count * windows * owned)
    same = lax.rem(lax.broadcasted_iota(jnp.int32, square, 0), owned) == lax.rem(
        lax.broadcasted_iota(jnp.int32, square, 1), owned
    )

    def across(window):
        own_q(window).wait()
        each_shift(lambda shift: copy_q(window, shift).wait())
        mixed = attend_heads(
            query_rows[window],
            lambda start, stop: key_rows[:, start:stop],
            lambda start, stop: value_rows[:, start:stop],
            same,
        )
        rows = jnp.dot(mixed, pw[...], preferred_element_type=jnp.float32) + pb_ref[...]
        proj[window] = rows.astype(jnp.bfloat16)
        own_r(window).start()
        each_shift(lambda shift: copy_r(window, shift).start())

    each_window(across)

    tokens_win = field.shape[1]
    tile = TILE_COLS

    def copy_to(source, target, sems, step_row, step_col):
        return pltpu.make_async_remote_copy(
            src_ref=source,
            dst_ref=target,
            send_sem=sems[0],
            recv_sem=sems[1],
            device_id={"row": my_row + step_row, "col": my_col + step_col},
            device_id_type=pl.DeviceIdType.MESH,
        )

    def edge(step, down):
        source = pl.ds(tokens_win - tile if down else 0, tile)
        target = halo_up if down else halo_down
        place = 0 if down else 1
        return copy_to(
            field.at[step, source, :],
            target.at[step],
            (edge_send.at[place, step], edge_recv.at[place, step]),
            1 if down else -1,
            0,
        )

    def side(right, step_row):
        target = side_left if right else side_right
        place = (0 if right else 3) + step_row + 1
        if step_row == 0:
            source, rows = (pl.ds(0, tokens_win), pl.ds(tile, tokens_win))
        elif step_row > 0:
            source, rows = (pl.ds(tokens_win - tile, tile), pl.ds(0, tile))
        else:
            source, rows = (pl.ds(0, tile), pl.ds(tokens_win + tile, tile))
        return copy_to(
            field.at[0, source, :],
            target.at[rows, :],
            (side_send.at[place], side_recv.at[place]),
            step_row,
            1 if right else -1,
        )

    row_ways = ((0, None, None), (1, has_down, has_up), (-1, has_up, has_down))

    def send_sides(right):
        there = has_right if right else has_left
        for step_row, goes, _ in row_ways:

            @pl.when(there if goes is None else there & goes)
            def _():
                side(right, step_row).start()

    def wait_sides(right):
        there, here = (has_right, has_left) if right else (has_left, has_right)
        for step_row, goes, comes in row_ways:

            @pl.when(there if goes is None else there & goes)
            def _():
                side(right, step_row).wait_send()

            @pl.when(here if comes is None else here & comes)
            def _():
                side(right, step_row).wait_recv()

    def finish(step):
        own_r(step).wait()
        each_shift(lambda shift: copy_r(step, shift).wait())
        for down, goes in ((True, has_down), (False, has_up)):

            @pl.when(goes)
            def _():
                edge(step, down).start()

    def wait_edges(step):
        for down, goes, comes in ((True, has_down, has_up), (False, has_up, has_down)):

            @pl.when(goes)
            def _():
                edge(step, down).wait_send()

            @pl.when(comes)
            def _():
                edge(step, down).wait_recv()

    depth = fk.shape[-1]
    high = tokens_win + 2 * tile
    size = high - tile
    column = lax.rem(lax.broadcasted_iota(jnp.int32, (high, depth), 0), tile)

    def lanes_of(parity):
        return slice(parity * 2 * depth, (parity + 1) * 2 * depth)

    def build(step):
        place = ordered(step) + 1
        for parity in range(2):
            lanes = lanes_of(parity)
            middle = slice(depth, 3 * depth)
            shuffled[parity, place, 0:tile, middle] = halo_up[step, :, lanes]
            shuffled[parity, place, tile : tile + tokens_win, middle] = field[step, :, lanes]
            shuffled[parity, place, tile + tokens_win :, middle] = halo_down[step, :, lanes]

    def shift_left(planes, parity, place):
        near = planes[parity, place, :, 2 * depth : 3 * depth].astype(jnp.float32)
        far = planes[parity, place - 1, :, 2 * depth : 3 * depth].astype(jnp.float32)
        moved = jnp.where(
            column == 0, pltpu.roll(far, high - (tile - 1), 0), pltpu.roll(near, 1, 0)
        )
        planes[parity, place, :, 0:depth] = moved.astype(jnp.bfloat16)

    def shift_right(planes, parity, place):
        near = planes[parity, place, :, depth : 2 * depth].astype(jnp.float32)
        far = planes[parity, place + 1, :, depth : 2 * depth].astype(jnp.float32)
        moved = jnp.where(
            column == tile - 1, pltpu.roll(far, tile - 1, 0), pltpu.roll(near, high - 1, 0)
        )
        planes[parity, place, :, 3 * depth : 4 * depth] = moved.astype(jnp.bfloat16)

    def shift(planes, steps):
        for step in steps:
            for parity in range(2):
                shift_left(planes, parity, ordered(step) + 1)
                shift_right(planes, parity, ordered(step) + 1)

    def convolve_rows(source, weights, row_parity, col_parity, places, start, length):
        if row_parity == 0:
            taps = ((1, -tile), (0, 0), (1, 0))
        else:
            taps = ((0, 0), (1, 0), (0, tile))
        result = None
        for tap, (parity, move) in enumerate(taps):
            cells = [
                source[
                    parity,
                    place,
                    start + move : start + move + length,
                    col_parity * depth : (col_parity + 3) * depth,
                ]
                for place in places
            ]
            cells = cells[0] if len(cells) == 1 else jnp.concatenate(cells, axis=0)
            part = jnp.dot(cells, weights[tap], preferred_element_type=jnp.float32)
            result = part if result is None else result + part
        return result

    line = lax.broadcasted_iota(jnp.int32, (size, depth), 0)
    line_stop = jnp.where(has_down, size, size - tile)
    line_start = jnp.where(has_up, 0, tile)

    def convolve_first(places, col_parities):
        for parity in range(2):
            start = tile if parity == 0 else 0
            valid = (line < line_stop) if parity == 0 else (line >= line_start)
            for other in col_parities:
                value = convolve_rows(shuffled, fk, parity, other, places, start, size)
                value = jax.nn.gelu(value + fb_ref[...])
                for index, place in enumerate(places):
                    kept = jnp.where(valid, value[index * size : (index + 1) * size], 0.0)
                    activated[
                        parity,
                        place,
                        start : start + size,
                        (other + 1) * depth : (other + 2) * depth,
                    ] = kept.astype(jnp.bfloat16)

    def convolve_second(steps):
        places = [ordered(step) + 1 for step in steps]
        for parity in range(2):
            for other in range(2):
                value = convolve_rows(activated, sk, parity, other, places, tile, tokens_win)
                value = (value + sb_ref[...]).astype(jnp.bfloat16)
                for index, place in enumerate(places):
                    begin = pl.multiple_of((place - 1) * tile, tile)
                    for row in range(tokens_win // tile):
                        at = index * tokens_win + row * tile
                        out_ref[
                            2 * row + parity,
                            pl.ds(begin, tile),
                            other * depth : (other + 1) * depth,
                        ] = value[at : at + tile]

    final = windows - 1
    finish(0)
    send_sides(False)
    send_sides(True)
    for step in range(1, final):
        finish(step)
    wait_sides(False)
    wait_sides(True)
    for parity in range(2):
        for place, source in ((0, side_left), (windows + 1, side_right)):
            shuffled[parity, place, :, depth : 3 * depth] = source[:, lanes_of(parity)]
    for step in range(final):
        wait_edges(step)
        build(step)

    early = list(range(final - 1))
    shift(shuffled, early)

    @pl.when(has_left)
    def _():
        for parity in range(2):
            shift_right(shuffled, parity, 0)
        convolve_first([0], (1,))

    @pl.when(has_right)
    def _():
        for parity in range(2):
            shift_left(shuffled, parity, windows + 1)
        convolve_first([windows + 1], (0,))

    convolve_first([ordered(step) + 1 for step in early], (0, 1))
    finish(final)
    shift(activated, early[:-1])
    convolve_second(early[:-1])
    wait_edges(final)
    build(final)
    late = [final - 1, final]
    shift(shuffled, late)
    convolve_first([ordered(step) + 1 for step in late], (0, 1))
    rest = early[-1:] + late
    shift(activated, rest)
    convolve_second(rest)


def fused(qw, kw, vw, qi, ki, proj_weight, proj_bias, first_kernel, first_bias, second_kernel, second_bias):
    windows, tokens_win, features = qw.shape
    count_row = lax.axis_size("row")
    count_col = lax.axis_size("col")
    count = count_row * count_col
    owned = tokens_win // count
    channels = proj_weight.shape[-1]
    depth = first_kernel.shape[-1]
    taps = (first_kernel.shape[0], first_kernel.shape[1] * first_kernel.shape[2], depth)
    token_rows = tokens_win // TILE_COLS
    planes = (2, windows + 2, tokens_win + 2 * TILE_COLS, 4 * depth)
    whole = pl.BlockSpec(memory_space=pl.ANY)
    held = pl.BlockSpec(memory_space=pltpu.VMEM)
    dma = pltpu.SemaphoreType.DMA
    return pl.pallas_call(
        functools.partial(attention_kernel, count_row, count_col),
        out_shape=jax.ShapeDtypeStruct(
            (2 * token_rows, windows * TILE_COLS, 2 * depth), jnp.bfloat16
        ),
        in_specs=[whole] * 8 + [held] * 3,
        out_specs=held,
        scratch_shapes=[
            pltpu.VMEM(qw.shape, jnp.bfloat16),
            pltpu.VMEM(qw.shape, jnp.bfloat16),
            pltpu.VMEM(qw.shape, jnp.bfloat16),
            pltpu.VMEM(proj_weight.shape, jnp.bfloat16),
            pltpu.VMEM(qw.shape, jnp.bfloat16),
            pltpu.VMEM((count, windows, owned, features), jnp.bfloat16),
            pltpu.VMEM((count, windows, owned, features), jnp.bfloat16),
            pltpu.VMEM((windows, count, owned, features), jnp.bfloat16),
            pltpu.VMEM((windows, tokens_win, channels), jnp.bfloat16),
            pltpu.VMEM((windows, tokens_win, channels), jnp.bfloat16),
            pltpu.VMEM(taps, jnp.bfloat16),
            pltpu.VMEM(taps, jnp.bfloat16),
            pltpu.VMEM((windows, TILE_COLS, channels), jnp.bfloat16),
            pltpu.VMEM((windows, TILE_COLS, channels), jnp.bfloat16),
            pltpu.VMEM((tokens_win + 2 * TILE_COLS, channels), jnp.bfloat16),
            pltpu.VMEM((tokens_win + 2 * TILE_COLS, channels), jnp.bfloat16),
            pltpu.VMEM(planes, jnp.bfloat16),
            pltpu.VMEM(planes, jnp.bfloat16),
            dma((6,)),
            dma((2,)),
            dma((windows,)),
            dma((windows,)),
            dma((count,)),
            dma((count,)),
            dma((count,)),
            dma((count,)),
            dma((windows, count)),
            dma((windows, count)),
            dma((windows, count)),
            dma((windows, count)),
            dma((2, windows)),
            dma((2, windows)),
            dma((6,)),
            dma((6,)),
        ],
        compiler_params=pltpu.CompilerParams(
            collective_id=0, has_side_effects=True, vmem_limit_bytes=62 * 1024 * 1024
        ),
    )(
        qw,
        kw,
        vw,
        qi,
        ki,
        proj_weight,
        first_kernel.reshape(taps),
        second_kernel.reshape(taps),
        proj_bias.reshape(1, channels),
        first_bias.reshape(1, depth),
        second_bias.reshape(1, depth),
    )


def convolutions(
    projected, rows_dev, cols_dev, first_kernel, first_bias, second_kernel, second_bias
):
    grouped = projected.reshape(rows_dev, cols_dev, TILE_ROWS, TILE_COLS, 2, 2, CHANNELS)
    shuffled = jnp.transpose(grouped, (0, 2, 4, 1, 3, 5, 6)).reshape(
        rows_dev * TILE_ROWS * 2, cols_dev * TILE_COLS * 2, CHANNELS
    )
    activated = jax.nn.gelu(convolve(shuffled, first_kernel, first_bias)).astype(jnp.bfloat16)
    return convolve(activated, second_kernel, second_bias).astype(jnp.bfloat16)


def shards(
    query_window,
    key_window,
    value_window,
    query_index,
    key_index,
    proj_weight,
    proj_bias,
    first_kernel,
    first_bias,
    second_kernel,
    second_bias,
):
    rows_dev, cols_dev, tokens_win, features = query_window.shape
    flat = (rows_dev * cols_dev, tokens_win, features)
    owners = lax.axis_size("row") * lax.axis_size("col")
    small = rows_dev == 1 and cols_dev > 2 and lax.axis_size("col") == 2
    if small and tokens_win % (owners * 8) == 0 and features % LANES == 0:
        fine = fused(
            query_window.reshape(flat),
            key_window.reshape(flat),
            value_window.reshape(flat),
            query_index.reshape(flat),
            key_index.reshape(flat),
            proj_weight,
            proj_bias,
            first_kernel,
            first_bias,
            second_kernel,
            second_bias,
        )
        return fine.reshape(fine.shape[0], 2 * fine.shape[1], -1)
    layout = (rows_dev * cols_dev, tokens_win, HEADS, HEAD_DIM)
    window_out = window_attend(
        query_window.reshape(layout), key_window.reshape(layout), value_window.reshape(layout)
    ).reshape(query_window.shape)
    count_row = lax.axis_size("row")
    count_col = lax.axis_size("col")
    owned_tokens = tokens_win // (count_row * count_col)
    moved = (
        lax.all_to_all(query_index, ("row", "col"), split_axis=2, concat_axis=0, tiled=True),
        lax.all_to_all(key_index, ("row", "col"), split_axis=2, concat_axis=0, tiled=True),
        lax.all_to_all(window_out, ("row", "col"), split_axis=2, concat_axis=0, tiled=True),
    )
    owner_shape = moved[0].shape
    across = (-1, owned_tokens, HEADS, HEAD_DIM)
    index_out = index_attend(
        moved[0].reshape(across), moved[1].reshape(across), moved[2].reshape(across)
    )
    index_rows = index_out.reshape(-1, features)
    owner_rows = (
        jnp.dot(index_rows, proj_weight, preferred_element_type=jnp.float32) + proj_bias
    ).astype(jnp.bfloat16)
    last = owner_rows.shape[-1]
    shaped = owner_rows.reshape(tuple(owner_shape[:-1]) + (last,))
    returned = lax.all_to_all(shaped, ("row", "col"), split_axis=0, concat_axis=2, tiled=True)
    projected = returned.reshape(rows_dev * cols_dev * tokens_win, last)
    return convolutions(
        projected, rows_dev, cols_dev, first_kernel, first_bias, second_kernel, second_bias
    )


def solution(mesh):
    in_specs = (
        P(("grp", "row"), "col", None, None),
        P(("grp", "row"), "col", None, None),
        P(("grp", "row"), "col", None, None),
        P(("grp", "row"), "col", None, None),
        P(("grp", "row"), "col", None, None),
        P(),
        P(),
        P(),
        P(),
        P(),
        P(),
    )
    out_specs = P(("grp", "row"), "col", None)
    return jax.shard_map(shards, mesh=mesh, in_specs=in_specs, out_specs=out_specs, check_vma=False)
```

```python
import functools
import math

import jax
import jax.numpy as jnp
from jax import lax
from jax.experimental import pallas as pl
from jax.experimental.pallas import tpu as pltpu
from jax.sharding import PartitionSpec as P

HEADS = 8
HEAD_DIM = 160
CHANNELS = 256
TILE_ROWS = 8
TILE_COLS = 16
LANES = 128


def extended(value, sides, width):
    for axis, dim in sides:
        size, length = (lax.axis_size(axis), value.shape[dim])
        up = [(i, (i + 1) % size) for i in range(size - 1)]
        down = [(j, i) for i, j in up]
        last = lax.slice_in_dim(value, length - width, length, axis=dim)
        first = lax.slice_in_dim(value, 0, width, axis=dim)
        before = lax.ppermute(last, axis, up)
        after = lax.ppermute(first, axis, down)
        value = jnp.concatenate([before, value, after], axis=dim)
    return value


def softmax_rows(scores):
    highest = jnp.max(scores, axis=-1, keepdims=True)
    raised = jnp.exp(scores - highest)
    return (raised / jnp.sum(raised, axis=-1, keepdims=True)).astype(jnp.bfloat16)


def window_attend(queries, key_rows, values):
    scores = jnp.einsum(
        "blhd,bmhd->bhlm", queries, key_rows, preferred_element_type=jnp.float32
    ) / math.sqrt(HEAD_DIM)
    weights = softmax_rows(scores)
    return jnp.einsum(
        "bhlm,bmhd->blhd", weights, values, preferred_element_type=jnp.float32
    ).astype(jnp.bfloat16)


def index_attend(queries, key_rows, values):
    scores = jnp.einsum(
        "lbhd,mbhd->bhlm", queries, key_rows, preferred_element_type=jnp.float32
    ) / math.sqrt(HEAD_DIM)
    weights = softmax_rows(scores)
    return jnp.einsum(
        "bhlm,mbhd->lbhd", weights, values, preferred_element_type=jnp.float32
    ).astype(jnp.bfloat16)


def convolve(image, kernel, bias):
    height, breadth, depth = image.shape
    padded = extended(image, (("row", 0), ("col", 1)), 1)
    total = jnp.zeros((height * breadth, kernel.shape[-1]), jnp.float32)
    for row_shift in range(3):
        for col_shift in range(3):
            cells = padded[row_shift : row_shift + height, col_shift : col_shift + breadth].reshape(
                -1, depth
            )
            total = total + jnp.dot(
                cells, kernel[row_shift, col_shift], preferred_element_type=jnp.float32
            )
    return (total + bias).reshape(height, breadth, -1)


def attend_heads(queries, key_part, value_part, same):
    rows, features = queries.shape
    head_dim = features // HEADS
    factor = math.log2(math.e) / math.sqrt(head_dim)
    blocks = [None] * (features // LANES)
    for head in range(HEADS):
        low, high = (head * head_dim, (head + 1) * head_dim)
        start, stop = (low // LANES * LANES, -(-high // LANES) * LANES)
        lane = lax.broadcasted_iota(jnp.int32, (rows, stop - start), 1) + start
        inside = (lane >= low) & (lane < high)
        part = queries[:, start:stop]
        part = jnp.where(inside, part, jnp.zeros_like(part))
        scores = lax.dot_general(
            part,
            key_part(start, stop),
            (((1,), (1,)), ((), ())),
            preferred_element_type=jnp.float32,
        )
        if same is not None:
            scores = jnp.where(same, scores, -1e30)
        highest = jnp.max(scores, axis=-1, keepdims=True)
        raised = jnp.exp2((scores - highest) * factor)
        weights = (raised * (1.0 / jnp.sum(raised, axis=-1, keepdims=True))).astype(jnp.bfloat16)
        mixed = jnp.dot(weights, value_part(start, stop), preferred_element_type=jnp.float32)
        mixed = jnp.where(inside, mixed, 0.0)
        for block in range(start // LANES, stop // LANES):
            piece = mixed[:, block * LANES - start : (block + 1) * LANES - start]
            blocks[block] = piece if blocks[block] is None else blocks[block] + piece
    return jnp.concatenate(blocks, axis=1).astype(jnp.bfloat16)


def attention_kernel(
    count_row,
    count_col,
    qw_hbm,
    kw_hbm,
    vw_hbm,
    qi_hbm,
    ki_hbm,
    pw_hbm,
    fk_hbm,
    sk_hbm,
    pb_ref,
    fb_ref,
    sb_ref,
    out_ref,
    qw,
    kw,
    vw,
    pw,
    window_out,
    k_all,
    v_all,
    q_all,
    proj,
    field,
    fk,
    sk,
    halo_up,
    halo_down,
    side_right,
    side_left,
    shuffled,
    activated,
    load_sem,
    own_sem,
    q_own_sem,
    out_own_sem,
    k_send,
    k_recv,
    v_send,
    v_recv,
    q_send,
    q_recv,
    r_send,
    r_recv,
    edge_send,
    edge_recv,
    side_send,
    side_recv,
):
    count = count_row * count_col
    windows = qw.shape[0]
    owned = k_all.shape[2]
    features = qw.shape[2]
    me = lax.axis_index("row") * count_col + lax.axis_index("col")

    def offset(step):
        half = (step + 1) // 2
        return count // 2 + jnp.where(step % 2 == 1, half, -half)

    def peer_of(shift):
        return lax.rem(me + shift, count)

    def device(peer):
        return {"row": peer // count_col, "col": lax.rem(peer, count_col)}

    def tokens(peer):
        return pl.ds(pl.multiple_of(peer * owned, owned), owned)

    def copy_k(shift):
        peer = peer_of(shift)
        return pltpu.make_async_remote_copy(
            src_ref=ki_hbm.at[:, tokens(peer), :],
            dst_ref=k_all.at[me],
            send_sem=k_send.at[shift],
            recv_sem=k_recv.at[shift],
            device_id=device(peer),
            device_id_type=pl.DeviceIdType.MESH,
        )

    def copy_v(shift):
        peer = peer_of(shift)
        return pltpu.make_async_remote_copy(
            src_ref=window_out.at[:, tokens(peer), :],
            dst_ref=v_all.at[me],
            send_sem=v_send.at[shift],
            recv_sem=v_recv.at[shift],
            device_id=device(peer),
            device_id_type=pl.DeviceIdType.MESH,
        )

    def copy_q(window, shift):
        peer = peer_of(shift)
        return pltpu.make_async_remote_copy(
            src_ref=qi_hbm.at[window, tokens(peer), :],
            dst_ref=q_all.at[window, me],
            send_sem=q_send.at[window, shift],
            recv_sem=q_recv.at[window, shift],
            device_id=device(peer),
            device_id_type=pl.DeviceIdType.MESH,
        )

    def copy_r(window, shift):
        peer = peer_of(shift)
        return pltpu.make_async_remote_copy(
            src_ref=proj.at[window, tokens(peer), :],
            dst_ref=field.at[window, tokens(me), :],
            send_sem=r_send.at[window, shift],
            recv_sem=r_recv.at[window, shift],
            device_id=device(peer),
            device_id_type=pl.DeviceIdType.MESH,
        )

    def own_q(window):
        return pltpu.make_async_copy(
            qi_hbm.at[window, tokens(me), :], q_all.at[window, me], q_own_sem.at[window]
        )

    def own_r(window):
        return pltpu.make_async_copy(
            proj.at[window, tokens(me), :],
            field.at[window, tokens(me), :],
            out_own_sem.at[window],
        )

    loads = [
        pltpu.make_async_copy(source, target, load_sem.at[place])
        for place, (source, target) in enumerate(
            (
                (qw_hbm, qw),
                (kw_hbm, kw),
                (vw_hbm, vw),
                (pw_hbm, pw),
                (fk_hbm, fk),
                (sk_hbm, sk),
            )
        )
    ]
    for load in loads:
        load.start()
    own_k = pltpu.make_async_copy(ki_hbm.at[:, tokens(me), :], k_all.at[me], own_sem.at[0])
    own_k.start()

    def each_shift(body):
        def step(index, carry):
            body(offset(index))
            return carry

        lax.fori_loop(0, count - 1, step, 0)

    def each_window(body):
        def step(index, carry):
            body(index)
            return carry

        lax.fori_loop(0, windows, step, 0)

    each_window(lambda window: own_q(window).start())
    for halo in (halo_up, halo_down, side_right, side_left):
        halo[...] = jnp.zeros_like(halo)

    barrier = pltpu.get_barrier_semaphore()

    def greet(shift):
        pl.semaphore_signal(
            barrier,
            inc=1,
            device_id=device(peer_of(shift)),
            device_id_type=pl.DeviceIdType.MESH,
        )

    each_shift(greet)
    pl.semaphore_wait(barrier, count - 1)
    each_shift(lambda shift: copy_k(shift).start())

    def send_q(first, stop):
        def step(window, carry):
            each_shift(lambda shift: copy_q(window, shift).start())
            return carry

        lax.fori_loop(first, stop, step, 0)

    send_q(0, windows // 2)

    for load in loads:
        load.wait()

    def within(window):
        window_out[window] = attend_heads(
            qw[window],
            lambda start, stop: kw[window, :, start:stop],
            lambda start, stop: vw[window, :, start:stop],
            None,
        )

    each_window(within)
    own_v = pltpu.make_async_copy(
        window_out.at[:, tokens(me), :], v_all.at[me], own_sem.at[1]
    )
    own_v.start()
    each_shift(lambda shift: copy_v(shift).start())
    send_q(windows // 2, windows)

    own_k.wait()
    own_v.wait()
    each_shift(lambda shift: copy_k(shift).wait())
    each_shift(lambda shift: copy_v(shift).wait())

    key_rows = k_all.reshape(count * windows * owned, features)
    value_rows = v_all.reshape(count * windows * owned, features)
    query_rows = q_all.reshape(windows, count * owned, features)
    square = (count * owned, count * windows * owned)
    same = lax.rem(lax.broadcasted_iota(jnp.int32, square, 0), owned) == lax.rem(
        lax.broadcasted_iota(jnp.int32, square, 1), owned
    )

    def across(window):
        own_q(window).wait()
        each_shift(lambda shift: copy_q(window, shift).wait())
        mixed = attend_heads(
            query_rows[window],
            lambda start, stop: key_rows[:, start:stop],
            lambda start, stop: value_rows[:, start:stop],
            same,
        )
        rows = jnp.dot(mixed, pw[...], preferred_element_type=jnp.float32) + pb_ref[...]
        proj[window] = rows.astype(jnp.bfloat16)
        own_r(window).start()
        each_shift(lambda shift: copy_r(window, shift).start())

    each_window(across)

    my_row, my_col = (lax.axis_index("row"), lax.axis_index("col"))
    has_up, has_down = (my_row > 0, my_row < count_row - 1)
    has_left, has_right = (my_col > 0, my_col < count_col - 1)
    tokens_win = field.shape[1]
    tile = TILE_COLS

    def copy_to(source, target, sems, step_row, step_col):
        return pltpu.make_async_remote_copy(
            src_ref=source,
            dst_ref=target,
            send_sem=sems[0],
            recv_sem=sems[1],
            device_id={"row": my_row + step_row, "col": my_col + step_col},
            device_id_type=pl.DeviceIdType.MESH,
        )

    def edge(window, down):
        source = pl.ds(tokens_win - tile if down else 0, tile)
        target = halo_up if down else halo_down
        place = 0 if down else 1
        return copy_to(
            field.at[window, source, :],
            target.at[window],
            (edge_send.at[place, window], edge_recv.at[place, window]),
            1 if down else -1,
            0,
        )

    def side(right, step_row):
        window = windows - 1 if right else 0
        target = side_left if right else side_right
        place = (0 if right else 3) + step_row + 1
        if step_row == 0:
            source, rows = (pl.ds(0, tokens_win), pl.ds(tile, tokens_win))
        elif step_row > 0:
            source, rows = (pl.ds(tokens_win - tile, tile), pl.ds(0, tile))
        else:
            source, rows = (pl.ds(0, tile), pl.ds(tokens_win + tile, tile))
        return copy_to(
            field.at[window, source, :],
            target.at[rows, :],
            (side_send.at[place], side_recv.at[place]),
            step_row,
            1 if right else -1,
        )

    row_ways = ((0, None, None), (1, has_down, has_up), (-1, has_up, has_down))

    def send_sides(right):
        there = has_right if right else has_left
        for step_row, goes, _ in row_ways:

            @pl.when(there if goes is None else there & goes)
            def _():
                side(right, step_row).start()

    def finish(window):
        own_r(window).wait()
        each_shift(lambda shift: copy_r(window, shift).wait())
        for down, goes in ((True, has_down), (False, has_up)):

            @pl.when(goes)
            def _():
                edge(window, down).start()

    finish(0)
    send_sides(False)

    def later(window, carry):
        finish(window)
        return carry

    lax.fori_loop(1, windows, later, 0)
    send_sides(True)

    depth = fk.shape[-1]
    width = (windows + 1) * tile
    token_rows = tokens_win // tile
    total = shuffled.shape[1]

    for window in range(windows):
        for line in range(token_rows):
            start = tile + (line + 1) * width + window * tile
            for parity in range(2):
                shuffled[parity, start : start + tile, depth : 3 * depth] = field[
                    window,
                    line * tile : (line + 1) * tile,
                    parity * 2 * depth : (parity + 1) * 2 * depth,
                ]

    for window in range(windows):
        for down, goes, comes in ((True, has_down, has_up), (False, has_up, has_down)):

            @pl.when(goes)
            def _():
                edge(window, down).wait_send()

            @pl.when(comes)
            def _():
                edge(window, down).wait_recv()

    for right in (True, False):
        there, here = (has_right, has_left) if right else (has_left, has_right)
        for step_row, goes, comes in row_ways:

            @pl.when(there if goes is None else there & goes)
            def _():
                side(right, step_row).wait_send()

            @pl.when(here if comes is None else here & comes)
            def _():
                side(right, step_row).wait_recv()

    for parity in range(2):
        lanes = slice(parity * 2 * depth, (parity + 1) * 2 * depth)
        for window in range(windows):
            for source, line in ((halo_up, 0), (halo_down, token_rows + 1)):
                start = tile + line * width + window * tile
                shuffled[parity, start : start + tile, depth : 3 * depth] = source[
                    window, :, lanes
                ]
        first = lax.broadcasted_iota(jnp.int32, (tile, 2 * depth), 0) < tile // 2
        shuffled[parity, 0:tile, depth : 3 * depth] = side_left[0:tile, lanes]
        for line in range(token_rows + 2):
            start = tile + line * width + windows * tile
            block = side_right[line * tile : (line + 1) * tile, lanes]
            if line < token_rows + 1:
                after = side_left[(line + 1) * tile : (line + 2) * tile, lanes]
                block = jnp.where(first, block, after)
            shuffled[parity, start : start + tile, depth : 3 * depth] = block
        odd = shuffled[parity, :, 2 * depth : 3 * depth].astype(jnp.float32)
        shuffled[parity, :, 0:depth] = pltpu.roll(odd, 1, 0).astype(jnp.bfloat16)
        even = shuffled[parity, :, depth : 2 * depth].astype(jnp.float32)
        shuffled[parity, :, 3 * depth :] = pltpu.roll(even, total - 1, 0).astype(jnp.bfloat16)

    def convolve_rows(source, weights, row_parity, col_parity, start, size):
        if row_parity == 0:
            taps = ((1, -width), (0, 0), (1, 0))
        else:
            taps = ((0, 0), (1, 0), (0, width))
        result = None
        for tap, (parity, shift) in enumerate(taps):
            cells = source[
                parity,
                start + shift : start + shift + size,
                col_parity * depth : (col_parity + 3) * depth,
            ]
            part = jnp.dot(cells, weights[tap], preferred_element_type=jnp.float32)
            result = part if result is None else result + part
        return result

    size = total - width
    main = windows * tile
    right_stop = jnp.where(has_right, main + tile // 2, main)
    left_start = jnp.where(has_left, main + tile // 2, width)
    line_start = jnp.where(has_up, 0, 1)
    line_stop = jnp.where(has_down, token_rows + 2, token_rows + 1)
    for parity in range(2):
        start = width if parity == 0 else 0
        place = lax.broadcasted_iota(jnp.int32, (size, depth), 0) + start
        column = lax.rem(place + (width - tile), width)
        line = lax.div(place + (width - tile) + tile // 2, width) - 1
        valid = (column < right_stop) | (column >= left_start)
        valid = valid & ((line < line_stop) if parity == 0 else (line >= line_start))
        for other in range(2):
            value = convolve_rows(shuffled, fk, parity, other, start, size) + fb_ref[...]
            value = jnp.where(valid, jax.nn.gelu(value), 0.0)
            rows = slice(start, start + size)
            activated[parity, rows, (other + 1) * depth : (other + 2) * depth] = value.astype(
                jnp.bfloat16
            )
            if other == 1:
                moved = pltpu.roll(value, 1, 0)
                activated[parity, rows, 0:depth] = moved.astype(jnp.bfloat16)
            else:
                moved = pltpu.roll(value, size - 1, 0)
                activated[parity, rows, 3 * depth :] = moved.astype(jnp.bfloat16)

    for parity in range(2):
        for other in range(2):
            value = convolve_rows(
                activated, sk, parity, other, tile + width, token_rows * width
            )
            value = (value + sb_ref[...]).astype(jnp.bfloat16)
            for line in range(token_rows):
                out_ref[2 * line + parity, :, other * depth : (other + 1) * depth] = value[
                    line * width : line * width + windows * tile
                ]


def fused(qw, kw, vw, qi, ki, proj_weight, proj_bias, first_kernel, first_bias, second_kernel, second_bias):
    windows, tokens_win, features = qw.shape
    count_row = lax.axis_size("row")
    count_col = lax.axis_size("col")
    count = count_row * count_col
    owned = tokens_win // count
    channels = proj_weight.shape[-1]
    depth = first_kernel.shape[-1]
    taps = (first_kernel.shape[0], first_kernel.shape[1] * first_kernel.shape[2], depth)
    token_rows = tokens_win // TILE_COLS
    width = (windows + 1) * TILE_COLS
    planes = (2, TILE_COLS + (token_rows + 2) * width, 4 * depth)
    whole = pl.BlockSpec(memory_space=pl.ANY)
    held = pl.BlockSpec(memory_space=pltpu.VMEM)
    dma = pltpu.SemaphoreType.DMA
    return pl.pallas_call(
        functools.partial(attention_kernel, count_row, count_col),
        out_shape=jax.ShapeDtypeStruct(
            (2 * token_rows, windows * TILE_COLS, 2 * depth), jnp.bfloat16
        ),
        in_specs=[whole] * 8 + [held] * 3,
        out_specs=held,
        scratch_shapes=[
            pltpu.VMEM(qw.shape, jnp.bfloat16),
            pltpu.VMEM(qw.shape, jnp.bfloat16),
            pltpu.VMEM(qw.shape, jnp.bfloat16),
            pltpu.VMEM(proj_weight.shape, jnp.bfloat16),
            pltpu.VMEM(qw.shape, jnp.bfloat16),
            pltpu.VMEM((count, windows, owned, features), jnp.bfloat16),
            pltpu.VMEM((count, windows, owned, features), jnp.bfloat16),
            pltpu.VMEM((windows, count, owned, features), jnp.bfloat16),
            pltpu.VMEM((windows, tokens_win, channels), jnp.bfloat16),
            pltpu.VMEM((windows, tokens_win, channels), jnp.bfloat16),
            pltpu.VMEM(taps, jnp.bfloat16),
            pltpu.VMEM(taps, jnp.bfloat16),
            pltpu.VMEM((windows, TILE_COLS, channels), jnp.bfloat16),
            pltpu.VMEM((windows, TILE_COLS, channels), jnp.bfloat16),
            pltpu.VMEM((tokens_win + 2 * TILE_COLS, channels), jnp.bfloat16),
            pltpu.VMEM((tokens_win + 2 * TILE_COLS, channels), jnp.bfloat16),
            pltpu.VMEM(planes, jnp.bfloat16),
            pltpu.VMEM(planes, jnp.bfloat16),
            dma((6,)),
            dma((2,)),
            dma((windows,)),
            dma((windows,)),
            dma((count,)),
            dma((count,)),
            dma((count,)),
            dma((count,)),
            dma((windows, count)),
            dma((windows, count)),
            dma((windows, count)),
            dma((windows, count)),
            dma((2, windows)),
            dma((2, windows)),
            dma((6,)),
            dma((6,)),
        ],
        compiler_params=pltpu.CompilerParams(
            collective_id=0, has_side_effects=True, vmem_limit_bytes=62 * 1024 * 1024
        ),
    )(
        qw,
        kw,
        vw,
        qi,
        ki,
        proj_weight,
        first_kernel.reshape(taps),
        second_kernel.reshape(taps),
        proj_bias.reshape(1, channels),
        first_bias.reshape(1, depth),
        second_bias.reshape(1, depth),
    )


def convolutions(
    projected, rows_dev, cols_dev, first_kernel, first_bias, second_kernel, second_bias
):
    grouped = projected.reshape(rows_dev, cols_dev, TILE_ROWS, TILE_COLS, 2, 2, CHANNELS)
    shuffled = jnp.transpose(grouped, (0, 2, 4, 1, 3, 5, 6)).reshape(
        rows_dev * TILE_ROWS * 2, cols_dev * TILE_COLS * 2, CHANNELS
    )
    activated = jax.nn.gelu(convolve(shuffled, first_kernel, first_bias)).astype(jnp.bfloat16)
    return convolve(activated, second_kernel, second_bias).astype(jnp.bfloat16)


def shards(
    query_window,
    key_window,
    value_window,
    query_index,
    key_index,
    proj_weight,
    proj_bias,
    first_kernel,
    first_bias,
    second_kernel,
    second_bias,
):
    rows_dev, cols_dev, tokens_win, features = query_window.shape
    flat = (rows_dev * cols_dev, tokens_win, features)
    owners = lax.axis_size("row") * lax.axis_size("col")
    if rows_dev == 1 and tokens_win % (owners * 8) == 0 and features % LANES == 0:
        fine = fused(
            query_window.reshape(flat),
            key_window.reshape(flat),
            value_window.reshape(flat),
            query_index.reshape(flat),
            key_index.reshape(flat),
            proj_weight,
            proj_bias,
            first_kernel,
            first_bias,
            second_kernel,
            second_bias,
        )
        return fine.reshape(fine.shape[0], 2 * fine.shape[1], -1)
    layout = (rows_dev * cols_dev, tokens_win, HEADS, HEAD_DIM)
    window_out = window_attend(
        query_window.reshape(layout), key_window.reshape(layout), value_window.reshape(layout)
    ).reshape(query_window.shape)
    count_row = lax.axis_size("row")
    count_col = lax.axis_size("col")
    owned_tokens = tokens_win // (count_row * count_col)
    moved = (
        lax.all_to_all(query_index, ("row", "col"), split_axis=2, concat_axis=0, tiled=True),
        lax.all_to_all(key_index, ("row", "col"), split_axis=2, concat_axis=0, tiled=True),
        lax.all_to_all(window_out, ("row", "col"), split_axis=2, concat_axis=0, tiled=True),
    )
    owner_shape = moved[0].shape
    across = (-1, owned_tokens, HEADS, HEAD_DIM)
    index_out = index_attend(
        moved[0].reshape(across), moved[1].reshape(across), moved[2].reshape(across)
    )
    index_rows = index_out.reshape(-1, features)
    owner_rows = (
        jnp.dot(index_rows, proj_weight, preferred_element_type=jnp.float32) + proj_bias
    ).astype(jnp.bfloat16)
    last = owner_rows.shape[-1]
    shaped = owner_rows.reshape(tuple(owner_shape[:-1]) + (last,))
    returned = lax.all_to_all(shaped, ("row", "col"), split_axis=0, concat_axis=2, tiled=True)
    projected = returned.reshape(rows_dev * cols_dev * tokens_win, last)
    return convolutions(
        projected, rows_dev, cols_dev, first_kernel, first_bias, second_kernel, second_bias
    )


def solution(mesh):
    in_specs = (
        P(("grp", "row"), "col", None, None),
        P(("grp", "row"), "col", None, None),
        P(("grp", "row"), "col", None, None),
        P(("grp", "row"), "col", None, None),
        P(("grp", "row"), "col", None, None),
        P(),
        P(),
        P(),
        P(),
        P(),
        P(),
    )
    out_specs = P(("grp", "row"), "col", None)
    return jax.shard_map(shards, mesh=mesh, in_specs=in_specs, out_specs=out_specs, check_vma=False)
```
